32 devices in a mesh: section: 4 (over z), seq: 8 (over y, x, core).
Axes of the slice: x: 2, y: 2, z: 4, core: 2. Of those that a mesh axis runs over, the one named last changes fastest.
Arguments:
- input_in_transit: bfloat16 [4, 1024, 4096], P('section', 'seq'), may hold values from -6 to 6
- mixer_norm_gain: float32 [4, 4096], P('section'), may hold values from 0.5 to 1.5
- convolution_weight: float32 [4, 4, 4096], P('section'), may hold values from -3 to 3
- convolution_bias: float32 [4, 4096], P('section'), may hold values from -2 to 2
- input_projection: bfloat16 [4, 4096, 288], P('section', 'seq'), may hold values from -0.09375 to 0.09375
- step_size_projection: bfloat16 [4, 256, 4096], P('section', None, 'seq'), may hold values from -0.375 to 0.375
- step_size_bias: float32 [4, 4096], P('section'), may hold values from -6.9 to -2.3
- log_decay_rates: float32 [4, 4096, 16], P('section'), may hold values from 0 to 2.77
- mixer_skip_weight: float32 [4, 4096], P('section'), may hold values from 0.5 to 1.5
- expert_norm_gain: float32 [4, 4096], P('section'), may hold values from 0.1 to 1.9
- router: bfloat16 [4, 4096, 16], P('section'), may hold values from -0.09375 to 0.09375
- gate_weight: bfloat16 [4, 4096, 12288], P('section', None, 'seq'), may hold values from -0.09375 to 0.09375
- up_weight: bfloat16 [4, 4096, 12288], P('section', None, 'seq'), may hold values from -0.09375 to 0.09375
- down_weight: bfloat16 [4, 12288, 4096], P('section', 'seq'), may hold values from -0.0546875 to 0.0546875
- expert_index_table: int32 [2, 4, 1024, 2], P(None, 'section', 'seq'), may hold values from 0 to 15, as said below
Outputs:
- layer_out: bfloat16 [4, 1024, 4096], P('section', 'seq')
The draws below stay inside these ranges and needn't reach their ends.
Inputs may be any that keep to these rules, and one draw needn't show every extreme that they name: `expert_index_table`: each token names two different experts of the 16; for each step and section, expert 0 is named by at most 8 tokens of any one block of 128 tokens.
All inputs are finite; a program needn't handle non-finite values.
Results may differ from the reference program's by a relative error of at most 0.0086.
Values may be sent and summed in bfloat16 or wider, within the bound.
A program may use at most 128 MiB of HBM per device.

```python
import jax
import jax.numpy as jnp
from jax import lax

MODEL_DIM = 4096
NSTATE = 16
RANK = 256
KCONV = 4
FF = 12288
EXPERTS = 16
STEPS = 2
L_DEV = 128
SEQUENCE_LENGTH = 1024
CAP = 8
N_SECTION = 4
N_SEQ = 8


def draw_expert_index_table(key, part):
    block_total = STEPS * N_SECTION * (SEQUENCE_LENGTH // L_DEV)
    keys = jax.random.split(jax.random.fold_in(key, 7321), 7)
    counts = jax.random.randint(keys[0], (block_total,), CAP // 4, CAP + 1)
    full = jax.random.randint(keys[1], (block_total,), 0, 4) == 0
    forced = jax.random.randint(keys[2], (), 0, block_total)
    full = full | (jnp.arange(block_total, dtype=jnp.int32) == forced)
    counts = jnp.where(full, CAP, counts)
    scores = jax.random.randint(keys[3], (block_total, L_DEV), 0, 1 << 20) * L_DEV + jnp.arange(L_DEV, dtype=jnp.int32)[None, :]
    order = jnp.argsort(scores, axis=1, stable=True)
    ranks = jnp.argsort(order, axis=1, stable=True)
    chosen = ranks < counts[:, None]
    first = jax.random.randint(keys[4], (block_total, L_DEV), 1, EXPERTS)
    offset = jax.random.randint(keys[5], (block_total, L_DEV), 1, EXPERTS - 1)
    second = 1 + (first - 1 + offset) % (EXPERTS - 1)
    side = jax.random.randint(keys[6], (block_total, L_DEV), 0, 2)
    first = jnp.where(chosen & (side == 0), 0, first)
    second = jnp.where(chosen & (side == 1), 0, second)
    pair = jnp.stack([first, second], -1).astype(jnp.int32)
    return pair.reshape(STEPS, N_SECTION, SEQUENCE_LENGTH, 2)


def block_levels(own_key, extent, pieces, smallest, largest):
    def one(axis_at, parts):
        draws = jax.random.uniform(jax.random.fold_in(jax.random.fold_in(own_key, 6), axis_at), (parts,), jnp.float32, smallest / len(pieces), largest / len(pieces))
        return jnp.repeat(jnp.exp(draws), extent[axis_at] // parts).reshape((-1,) + (1,) * (len(extent) - axis_at - 1))

    loudness = one(*pieces[0])
    for cut in pieces[1:]:
        loudness = loudness * one(*cut)
    return loudness


def centred(rng, shape, scale, limit, pieces=(), kind=jnp.bfloat16):
    values = scale * jax.random.normal(rng, shape, jnp.float32)
    if pieces:
        values = values * block_levels(rng, shape, pieces, -0.22, 0.18)
    return jnp.clip(values, -limit, limit).astype(kind)


def setup_inputs(seed: int = 0) -> dict:
    arg_keys = jax.random.split(jax.random.key(seed), 16)
    input_in_transit = centred(arg_keys[0], (N_SECTION, SEQUENCE_LENGTH, MODEL_DIM), 1.0, 6.0, ((0, 4), (1, 8)))
    mixer_norm_gain = jnp.clip(1.0 + 0.1 * jax.random.normal(arg_keys[1], (N_SECTION, MODEL_DIM), jnp.float32), 0.5, 1.5)
    convolution_weight = centred(arg_keys[2], (N_SECTION, KCONV, MODEL_DIM), 0.5, 3.0, ((0, 4),), jnp.float32)
    convolution_bias = centred(arg_keys[3], (N_SECTION, MODEL_DIM), 0.3, 2.0, ((0, 4),), jnp.float32)
    input_projection = centred(arg_keys[4], (N_SECTION, MODEL_DIM, RANK + 2 * NSTATE), MODEL_DIM ** -0.5, 0.09375, ((0, 4), (1, 8)))
    step_size_projection = centred(arg_keys[5], (N_SECTION, RANK, MODEL_DIM), RANK ** -0.5, 0.375, ((0, 4), (2, 8)))
    step_size_bias = jnp.clip(-6.9 + 4.6000001430511475 * jax.random.uniform(arg_keys[6], (N_SECTION, MODEL_DIM), jnp.float32) ** block_levels(arg_keys[6], (N_SECTION, MODEL_DIM), ((0, 4),), -0.2, 0.2), -6.9, -2.3)
    log_decay_rates = jnp.clip(2.77 * jax.random.uniform(arg_keys[7], (N_SECTION, MODEL_DIM, NSTATE), jnp.float32) ** block_levels(arg_keys[7], (N_SECTION, MODEL_DIM, NSTATE), ((0, 4),), -0.2, 0.2), 0.0, 2.77)
    mixer_skip_weight = jnp.clip(0.5 + 1.0 * jax.random.uniform(arg_keys[8], (N_SECTION, MODEL_DIM), jnp.float32) ** block_levels(arg_keys[8], (N_SECTION, MODEL_DIM), ((0, 4),), -0.2, 0.2), 0.5, 1.5)
    expert_norm_gain = jnp.clip(1.0 + 0.18 * jax.random.normal(arg_keys[9], (N_SECTION, MODEL_DIM), jnp.float32), 0.1, 1.9)
    router = centred(arg_keys[10], (N_SECTION, MODEL_DIM, EXPERTS), MODEL_DIM ** -0.5, 0.09375, ((0, 4),))
    gate_weight = centred(arg_keys[11], (N_SECTION, MODEL_DIM, FF), MODEL_DIM ** -0.5, 0.09375, ((0, 4), (2, 8)))
    up_weight = centred(arg_keys[12], (N_SECTION, MODEL_DIM, FF), MODEL_DIM ** -0.5, 0.09375, ((0, 4), (2, 8)))
    down_weight = centred(arg_keys[13], (N_SECTION, FF, MODEL_DIM), FF ** -0.5, 0.0546875, ((0, 4), (1, 8)))
    expert_index_table = draw_expert_index_table(jax.random.fold_in(arg_keys[15], 71), 0)
    return dict(input_in_transit=input_in_transit, mixer_norm_gain=mixer_norm_gain, convolution_weight=convolution_weight, convolution_bias=convolution_bias, input_projection=input_projection, step_size_projection=step_size_projection, step_size_bias=step_size_bias, log_decay_rates=log_decay_rates, mixer_skip_weight=mixer_skip_weight, expert_norm_gain=expert_norm_gain, router=router, gate_weight=gate_weight, up_weight=up_weight, down_weight=down_weight, expert_index_table=expert_index_table)


def rms_scale(values, gain):
    as_float = values.astype(jnp.float32)
    return as_float * lax.rsqrt(lax.optimization_barrier(jnp.mean(as_float * as_float, axis=-1, keepdims=True)) + 1e-06) * gain

def mixer(layer_input, mixer_norm_gain, convolution_weight, convolution_bias, input_projection, step_size_projection, step_size_bias, log_decay_rates, mixer_skip_weight):
    length = layer_input.shape[0]
    normed = rms_scale(layer_input, mixer_norm_gain).astype(jnp.bfloat16)
    padded = jnp.concatenate([jnp.zeros((KCONV - 1, MODEL_DIM), jnp.bfloat16), normed], 0)
    convolved = convolution_bias
    for tap in range(KCONV):
        convolved = convolved + convolution_weight[tap] * padded[tap:tap + length].astype(jnp.float32)
    inner = jax.nn.silu(convolved)
    inner_b = inner.astype(jnp.bfloat16)
    projected = jnp.dot(inner_b, input_projection, preferred_element_type=jnp.float32)
    low_rank = projected[:, :RANK].astype(jnp.bfloat16)
    b_in = projected[:, RANK:RANK + NSTATE]
    c_out = projected[:, RANK + NSTATE:]
    step_size = jax.nn.softplus(jnp.dot(low_rank, step_size_projection, preferred_element_type=jnp.float32) + step_size_bias)
    decay_rates = -jnp.exp(log_decay_rates)

    def advance(state, row_items):
        dt_row, in_row, b_row, c_row = row_items
        state = jnp.exp(dt_row[:, None] * decay_rates) * state + (dt_row * in_row)[:, None] * b_row[None, :]
        return (state, lax.optimization_barrier(jnp.sum(state * c_row[None, :], axis=1)))
    _, scanned = lax.scan(advance, jnp.zeros((MODEL_DIM, NSTATE), jnp.float32), (step_size, inner, b_in, c_out))
    return (layer_input.astype(jnp.float32) + (scanned + mixer_skip_weight * inner)).astype(jnp.bfloat16)

def experts_ref(mixed_rows, expert_norm_gain, router, gate_weight, up_weight, down_weight, chosen_ids):
    length = mixed_rows.shape[0]
    moe_in = rms_scale(mixed_rows, expert_norm_gain).astype(jnp.bfloat16)
    logits = jnp.dot(moe_in, router, preferred_element_type=jnp.float32)
    first = jnp.take_along_axis(logits, chosen_ids[:, 0:1], 1)[:, 0]
    second = jnp.take_along_axis(logits, chosen_ids[:, 1:2], 1)[:, 0]
    weight_one = jax.nn.sigmoid(first - second)
    weight_two = 1.0 - weight_one
    route_weight = jnp.where(chosen_ids[:, 0] == 0, weight_one, jnp.where(chosen_ids[:, 1] == 0, weight_two, jnp.zeros_like(weight_one)))
    routed = ((chosen_ids[:, 0] == 0) | (chosen_ids[:, 1] == 0)).astype(jnp.int32)
    blocked = routed.reshape(N_SEQ, L_DEV)
    slot = (jnp.cumsum(blocked, 1) - blocked).reshape(-1).astype(jnp.int32)
    block_of = (jnp.arange(length, dtype=jnp.int32) // L_DEV).astype(jnp.int32)
    total_slots = N_SEQ * CAP
    target = jnp.where(routed == 1, block_of * CAP + slot, total_slots).astype(jnp.int32)
    table = jnp.full((total_slots + 1,), length, jnp.int32).at[target].set(jnp.arange(length, dtype=jnp.int32))[:total_slots]
    padded_in = jnp.concatenate([moe_in, jnp.zeros((1, MODEL_DIM), jnp.bfloat16)], 0)
    sectioned = jnp.take(padded_in, table, axis=0)
    width = FF // N_SEQ

    def slice_term(total, index):
        start = (index * width).astype(jnp.int32)
        gate_cols = lax.dynamic_slice_in_dim(gate_weight, start, width, 1)
        up_cols = lax.dynamic_slice_in_dim(up_weight, start, width, 1)
        down_rows = lax.dynamic_slice_in_dim(down_weight, start, width, 0)
        gate_part = jnp.dot(sectioned, gate_cols, preferred_element_type=jnp.float32)
        up_part = jnp.dot(sectioned, up_cols, preferred_element_type=jnp.float32)
        hidden = (jax.nn.silu(gate_part) * up_part).astype(jnp.bfloat16)
        partial_value = jnp.dot(hidden, down_rows, preferred_element_type=jnp.float32).astype(jnp.bfloat16)
        partial_value = lax.optimization_barrier(partial_value)
        return (total + partial_value.astype(jnp.float32), None)
    summed, _ = lax.scan(slice_term, jnp.zeros((total_slots, MODEL_DIM), jnp.float32), jnp.arange(N_SEQ, dtype=jnp.int32))
    expert_out = summed.astype(jnp.bfloat16)
    padded_out = jnp.concatenate([expert_out, jnp.zeros((1, MODEL_DIM), jnp.bfloat16)], 0)
    picked = jnp.take(padded_out, target, axis=0).astype(jnp.float32)
    combined = route_weight[:, None] * picked
    return (mixed_rows.astype(jnp.float32) + combined).astype(jnp.bfloat16)

def reference(input_in_transit, mixer_norm_gain, convolution_weight, convolution_bias, input_projection, step_size_projection, step_size_bias, log_decay_rates, mixer_skip_weight, expert_norm_gain, router, gate_weight, up_weight, down_weight, expert_index_table):
    present_value = [input_in_transit[section_index] for section_index in range(N_SECTION)]
    produced = present_value
    for step in range(STEPS):
        produced = []
        for section_index in range(N_SECTION):
            mixed_rows = mixer(present_value[section_index], mixer_norm_gain[section_index], convolution_weight[section_index], convolution_bias[section_index], input_projection[section_index], step_size_projection[section_index], step_size_bias[section_index], log_decay_rates[section_index], mixer_skip_weight[section_index])
            produced.append(experts_ref(mixed_rows, expert_norm_gain[section_index], router[section_index], gate_weight[section_index], up_weight[section_index], down_weight[section_index], expert_index_table[step, section_index]))
        present_value = [produced[(section_index - 1) % N_SECTION] for section_index in range(N_SECTION)]
    return jnp.stack(produced, 0)
```

```python
import functools

import jax
import jax.numpy as jnp
from jax import lax
from jax.experimental import pallas as pl
from jax.experimental.pallas import tpu as pltpu
from jax.sharding import PartitionSpec as P

STEPS = 2
LANES = 128
ROWS = 8
LOG2E = 1.4426950408889634
MESH = pl.DeviceIdType.MESH
SMALL_VMEM = 8 * 1024 * 1024
MIX_VMEM = 24 * 1024 * 1024
PIECE = 16
AHEAD = 2


def greet(axis):
    n, me = lax.axis_size(axis), lax.axis_index(axis)
    barrier = pltpu.get_barrier_semaphore()
    for k in range(1, n):
        pl.semaphore_signal(
            barrier, inc=1, device_id={axis: lax.rem(me + k, n)}, device_id_type=MESH
        )
    pl.semaphore_wait(barrier, n - 1)


def exchange_kernel(axis, parts, *refs):
    n, me = lax.axis_size(axis), lax.axis_index(axis)
    count = len(parts)
    send_sem, recv_sem, local_sem = refs[2 * count :]
    greet(axis)
    copies = []
    for k in range(1, n):
        peer = lax.rem(me + k, n)
        for p, (src_at, dst_at) in enumerate(parts):
            copy = pltpu.make_async_remote_copy(
                src_ref=src_at(refs[p], peer),
                dst_ref=dst_at(refs[count + p], me),
                send_sem=send_sem.at[p, k],
                recv_sem=recv_sem.at[p, k],
                device_id={axis: peer},
                device_id_type=MESH,
            )
            copy.start()
            copies.append(copy)
    for p, (src_at, dst_at) in enumerate(parts):
        own = pltpu.make_async_copy(
            src_at(refs[p], me), dst_at(refs[count + p], me), local_sem.at[p]
        )
        own.start()
        copies.append(own)
    for copy in copies:
        copy.wait()


def exchange(xs, shapes, parts, axis, cid):
    n, count = lax.axis_size(axis), len(xs)
    return pl.pallas_call(
        functools.partial(exchange_kernel, axis, parts),
        out_shape=[jax.ShapeDtypeStruct(shape, x.dtype) for x, shape in zip(xs, shapes)],
        in_specs=[pl.BlockSpec(memory_space=pl.ANY)] * count,
        out_specs=[pl.BlockSpec(memory_space=pl.ANY)] * count,
        scratch_shapes=[
            pltpu.SemaphoreType.DMA((count, n)),
            pltpu.SemaphoreType.DMA((count, n)),
            pltpu.SemaphoreType.DMA((count,)),
        ],
        compiler_params=pltpu.CompilerParams(
            collective_id=cid, has_side_effects=True, vmem_limit_bytes=SMALL_VMEM
        ),
        name=f"exchange_{cid}",
    )(*xs)


def spread(axis, block, place, o_ref, send_sem, recv_sem, relay_send, relay_recv, local_sem):
    n, me = lax.axis_size(axis), lax.axis_index(axis)
    partner = me + 1 - 2 * lax.rem(me, 2)

    def send(source, at, target, sent, received):
        copy = pltpu.make_async_remote_copy(
            src_ref=source,
            dst_ref=place(o_ref, at),
            send_sem=sent,
            recv_sem=received,
            device_id={axis: target},
            device_id_type=MESH,
        )
        copy.start()
        return copy

    far = [
        send(block, me, lax.rem(me + 2 * k, n), send_sem.at[k], recv_sem.at[k])
        for k in range(1, n // 2)
    ]
    near = [send(block, me, partner, relay_send.at[0], relay_recv.at[0])]
    own = pltpu.make_async_copy(block, place(o_ref, me), local_sem)
    own.start()
    for k in range(1, n // 2):
        far[k - 1].wait_recv()
        source = lax.rem(me + n - 2 * k, n)
        near.append(
            send(place(o_ref, source), source, partner, relay_send.at[k], relay_recv.at[k])
        )
    for copy in far:
        copy.wait_send()
    for copy in near:
        copy.wait()
    own.wait()


def spread_scratch(n):
    return [pltpu.SemaphoreType.DMA((n // 2,))] * 4 + [pltpu.SemaphoreType.DMA]


def gather_kernel(axis, place, x_ref, o_ref, *sems):
    greet(axis)
    spread(axis, x_ref, place, o_ref, *sems)


def gather(x, shape, place, axis, cid):
    return pl.pallas_call(
        functools.partial(gather_kernel, axis, place),
        out_shape=jax.ShapeDtypeStruct(shape, x.dtype),
        in_specs=[pl.BlockSpec(memory_space=pl.ANY)],
        out_specs=pl.BlockSpec(memory_space=pl.ANY),
        scratch_shapes=spread_scratch(lax.axis_size(axis)),
        compiler_params=pltpu.CompilerParams(
            collective_id=cid, has_side_effects=True, vmem_limit_bytes=SMALL_VMEM
        ),
        name=f"gather_{cid}",
    )(x)


def reduce_here(axis, src_at, x_ref, held, send_sem, recv_sem, local_sem):
    n, me = lax.axis_size(axis), lax.axis_index(axis)
    copies = []
    for k in range(1, n):
        peer = lax.rem(me + k, n)
        copy = pltpu.make_async_remote_copy(
            src_ref=src_at(x_ref, peer),
            dst_ref=held.at[k],
            send_sem=send_sem.at[k],
            recv_sem=recv_sem.at[k],
            device_id={axis: peer},
            device_id_type=MESH,
        )
        copy.start()
        copies.append(copy)
    own = pltpu.make_async_copy(src_at(x_ref, me), held.at[0], local_sem)
    own.start()
    own.wait()
    total = held[0].astype(jnp.float32)
    for k in range(1, n):
        copies[k - 1].wait()
        total = total + held[k].astype(jnp.float32)
    return total


def reduce_scratch(n, shape, dtype):
    return [
        pltpu.VMEM((n,) + shape, dtype),
        pltpu.SemaphoreType.DMA((n,)),
        pltpu.SemaphoreType.DMA((n,)),
        pltpu.SemaphoreType.DMA,
    ]


def scatter_sum_kernel(axis, src_at, x_ref, o_ref, *scratch):
    greet(axis)
    o_ref[...] = reduce_here(axis, src_at, x_ref, *scratch)


def scatter_sum(x, shape, src_at, axis, cid):
    return pl.pallas_call(
        functools.partial(scatter_sum_kernel, axis, src_at),
        out_shape=jax.ShapeDtypeStruct(shape, jnp.float32),
        in_specs=[pl.BlockSpec(memory_space=pl.ANY)],
        out_specs=pl.BlockSpec(memory_space=pltpu.VMEM),
        scratch_shapes=reduce_scratch(lax.axis_size(axis), shape, x.dtype),
        compiler_params=pltpu.CompilerParams(
            collective_id=cid, has_side_effects=True, vmem_limit_bytes=SMALL_VMEM
        ),
        name=f"scatter_sum_{cid}",
    )(x)


def row_block(size):
    return lambda ref, i: ref.at[pl.ds(pl.multiple_of(i * size, size), size), :]


def column_block(size):
    return lambda ref, i: ref.at[:, pl.ds(pl.multiple_of(i * size, size), size)]


def whole(ref, i):
    return ref


def slot_of(ref, i):
    return ref.at[i]


def mixer_kernel(
    axis, nstate, low_ref, maps_ref, x_ref, p_ref, w_ref, bias_ref, a_ref, skip_ref, o_ref,
    full, bc, rs_low, rs_maps, dtb, vb, bb, cx, hb, yb, h_ref, ls, lr, ms, mr, gs, gr, bs, br,
):
    n, me = lax.axis_size(axis), lax.axis_index(axis)
    f32, bf16 = jnp.float32, jnp.bfloat16
    length, width = x_ref.shape
    span = PIECE * n
    blocks = length // span
    groups = nstate // ROWS
    wide = 2 * ROWS * nstate

    def to(peer, source, target, sent, received):
        return pltpu.make_async_remote_copy(
            src_ref=source,
            dst_ref=target,
            send_sem=sent,
            recv_sem=received,
            device_id={axis: peer},
            device_id_type=MESH,
        )

    def rows_of(j, device):
        return pl.ds(pl.multiple_of(j * span + device * PIECE, PIECE), PIECE)

    def lanes_of(j):
        return pl.ds(pl.multiple_of(j * span, span), span)

    def part_low(j, k):
        peer = lax.rem(me + k, n)
        return to(peer, low_ref.at[rows_of(j, peer), :], rs_low.at[j, k], ls.at[j, k], lr.at[j, k])

    def part_maps(j, sender):
        return to(j, maps_ref.at[:, lanes_of(j)], rs_maps.at[sender], ms.at[j], mr.at[sender])

    def sum_low(j, k):
        peer = lax.rem(me + k, n)
        mine = full.at[rows_of(j, me), :]
        return to(peer, mine, mine, gs.at[j, k], gr.at[j, k])

    def sum_maps(j, k):
        mine = bc.at[:, lanes_of(j)]
        return to(lax.rem(me + k, n), mine, mine, bs.at[k], br.at[j])

    def send_parts(j):
        @pl.when(me != j)
        def _():
            part_maps(j, me).start()

        for k in range(1, n):
            part_low(j, k).start()

    def reduce_and_send(j):
        total = low_ref[rows_of(j, me), :].astype(f32)
        for k in range(1, n):
            part_low(j, k).wait_recv()
            total = total + rs_low[j, k].astype(f32)
        full[rows_of(j, me), :] = total.astype(bf16)
        for k in range(1, n):
            sum_low(j, k).start()

        @pl.when(me == j)
        def _():
            maps = maps_ref[:, lanes_of(j)].astype(f32)
            for k in range(1, n):
                sender = lax.rem(me + k, n)
                part_maps(j, sender).wait_recv()
                maps = maps + rs_maps[sender].astype(f32)
            high = maps.astype(bf16)
            bc[: 2 * nstate, lanes_of(j)] = high
            bc[2 * nstate :, lanes_of(j)] = (maps - high.astype(f32)).astype(bf16)
            for k in range(1, n):
                sum_maps(j, k).start()

    spread_map = (
        lax.broadcasted_iota(jnp.int32, (nstate, wide), 1) % nstate
        == lax.broadcasted_iota(jnp.int32, (nstate, wide), 0)
    ).astype(bf16)
    own = (
        lax.broadcasted_iota(jnp.int32, (LANES, wide), 1) // nstate
        == lax.broadcasted_iota(jnp.int32, (LANES, wide), 0) % (2 * ROWS)
    )

    def chunk(start):
        here = pl.ds(pl.multiple_of(start, LANES), LANES)
        z = jnp.dot(full[here, :], w_ref[...], preferred_element_type=f32) + bias_ref[...]
        step = jnp.maximum(z, 0.0) + jnp.log1p(jnp.exp(-jnp.abs(z)))
        dtb[...] = step
        vb[...] = step * x_ref[here, :]
        maps = bc[: 2 * nstate, here].astype(f32) + bc[2 * nstate :, here].astype(f32)
        for k in range(LANES):
            bb[k * nstate : (k + 1) * nstate, :] = jnp.broadcast_to(
                maps[:nstate, k : k + 1], (nstate, LANES)
            )
        c = maps[nstate:]
        c_hi = c.astype(bf16)
        c_lo = (c - c_hi.astype(f32)).astype(bf16)
        for i, part in enumerate((c_hi, c_lo)):
            placed = lax.dot_general(
                part, spread_map, (((0,), (0,)), ((), ())), preferred_element_type=f32
            )
            cx[i] = jnp.where(own, placed, 0.0)
        rates = [a_ref[g * ROWS : (g + 1) * ROWS, :] for g in range(groups)]

        def tokens(i, states):
            states = list(states)
            base = pl.multiple_of(i * ROWS, ROWS)
            for k in range(ROWS):
                d = jnp.broadcast_to(dtb[pl.ds(base + k, 1), :], (ROWS, width))
                v = jnp.broadcast_to(vb[pl.ds(base + k, 1), :], (ROWS, width))
                row = pl.multiple_of((base + k) * nstate, nstate)
                for g in range(groups):
                    b = jnp.tile(bb[pl.ds(row + g * ROWS, ROWS), :], (1, width // LANES))
                    states[g] = jnp.exp2(d * rates[g]) * states[g] + v * b
                hb[pl.ds(row, nstate), :] = jnp.concatenate(states, 0).astype(bf16)
            return tuple(states)

        states = tuple(h_ref[g * ROWS : (g + 1) * ROWS, :] for g in range(groups))
        states = lax.fori_loop(0, LANES // ROWS, tokens, states)
        for g in range(groups):
            h_ref[g * ROWS : (g + 1) * ROWS, :] = states[g]
        for i in range(LANES // (2 * ROWS)):
            at = slice(i * 2 * ROWS, (i + 1) * 2 * ROWS)
            left = jnp.concatenate([cx[0, at, :], cx[1, at, :]], 0).astype(bf16)
            y = jnp.dot(left, hb[i * wide : (i + 1) * wide, :], preferred_element_type=f32)
            yb[at, :] = y[: 2 * ROWS] + y[2 * ROWS :]
        o_ref[here, :] = (
            p_ref[here, :].astype(f32) + (yb[...] + skip_ref[...] * x_ref[here, :])
        ).astype(bf16)

    h_ref[...] = jnp.zeros_like(h_ref)
    greet(axis)
    for j in range(AHEAD + 1):
        send_parts(j)
    for j in range(AHEAD):
        reduce_and_send(j)

    def block(j, carry):
        @pl.when(j + AHEAD + 1 < blocks)
        def _():
            send_parts(j + AHEAD + 1)

        @pl.when(j + AHEAD < blocks)
        def _():
            reduce_and_send(j + AHEAD)

        for k in range(1, n):
            sum_low(j, k).wait_recv()

        @pl.when(me != j)
        def _():
            sum_maps(j, 1).wait_recv()

        for i in range(span // LANES):
            chunk(j * span + i * LANES)
        return carry

    lax.fori_loop(0, blocks, block, 0)

    def finish(j, carry):
        @pl.when(me != j)
        def _():
            part_maps(j, me).wait_send()

        for k in range(1, n):
            part_low(j, k).wait_send()
            sum_low(j, k).wait_send()
        return carry

    lax.fori_loop(0, blocks, finish, 0)

    @pl.when(me < blocks)
    def _():
        for k in range(1, n):
            sum_maps(me, k).wait_send()


def mix(low, maps, x, present, w, bias, rates, skip, axis, cid):
    n = lax.axis_size(axis)
    length, width = x.shape
    nstate, rank = rates.shape[0], w.shape[0]
    span = PIECE * n
    blocks = length // span
    wide = 2 * ROWS * nstate
    f32, bf16 = jnp.float32, jnp.bfloat16
    dma = pltpu.SemaphoreType.DMA
    return pl.pallas_call(
        functools.partial(mixer_kernel, axis, nstate),
        out_shape=jax.ShapeDtypeStruct((length, width), bf16),
        in_specs=[pl.BlockSpec(memory_space=pltpu.VMEM)] * 8,
        out_specs=pl.BlockSpec(memory_space=pltpu.VMEM),
        scratch_shapes=[
            pltpu.VMEM((length, rank), bf16),
            pltpu.VMEM((4 * nstate, length), bf16),
            pltpu.VMEM((blocks, n, PIECE, rank), bf16),
            pltpu.VMEM((n, 2 * nstate, span), bf16),
            pltpu.VMEM((LANES, width), f32),
            pltpu.VMEM((LANES, width), f32),
            pltpu.VMEM((LANES * nstate, LANES), f32),
            pltpu.VMEM((2, LANES, wide), f32),
            pltpu.VMEM((LANES * nstate, width), bf16),
            pltpu.VMEM((LANES, width), f32),
            pltpu.VMEM((nstate, width), f32),
            dma((blocks, n)),
            dma((blocks, n)),
            dma((blocks,)),
            dma((n,)),
            dma((blocks, n)),
            dma((blocks, n)),
            dma((n,)),
            dma((blocks,)),
        ],
        compiler_params=pltpu.CompilerParams(
            collective_id=cid, has_side_effects=True, vmem_limit_bytes=MIX_VMEM
        ),
        cost_estimate=pl.CostEstimate(
            flops=6 * length * width * nstate,
            bytes_accessed=12 * length * width,
            transcendentals=length * width * nstate,
        ),
        name=f"mix_{cid}",
    )(low, maps, x, present, w, bias, rates, skip)


def passed_along(x, axis):
    length = lax.axis_size(axis)
    return lax.ppermute(x, axis, [(i, (i + 1) % length) for i in range(length)])


def dispatch_of(ids, blocks, capacity):
    length = ids.shape[0]
    size = length // blocks
    routed = (ids[:, 0] == 0) | (ids[:, 1] == 0)
    counted = routed.astype(jnp.float32).reshape(blocks, size)
    before = jnp.tril(jnp.ones((size, size), jnp.float32), -1)
    rank = jnp.dot(counted, before.T).reshape(length)
    slot = rank.astype(jnp.int32) + (jnp.arange(length, dtype=jnp.int32) // size) * capacity
    chosen = (jnp.arange(blocks * capacity, dtype=jnp.int32)[:, None] == slot[None, :]) & routed[
        None, :
    ]
    return chosen.astype(jnp.bfloat16), routed


def body(
    input_in_transit,
    mixer_norm_gain,
    convolution_weight,
    convolution_bias,
    input_projection,
    step_size_projection,
    step_size_bias,
    log_decay_rates,
    mixer_skip_weight,
    expert_norm_gain,
    router,
    gate_weight,
    up_weight,
    down_weight,
    expert_index_table,
):
    n, me = lax.axis_size("seq"), lax.axis_index("seq")
    experts = router.shape[2]
    rows = input_in_transit.shape[1]
    model = input_in_transit.shape[2]
    nstate = log_decay_rates.shape[2]
    rank = step_size_projection.shape[1]
    kernel = convolution_weight.shape[1]
    capacity = rows // 16
    length, width = rows * n, model // n
    slots = capacity * n
    f32, bf16 = jnp.float32, jnp.bfloat16

    def own(weight, axis):
        return lax.dynamic_slice_in_dim(weight, me * width, width, axis)

    gain = own(mixer_norm_gain[0], 0)
    taps = own(convolution_weight[0], 1)
    conv_bias = own(convolution_bias[0], 0)
    dt_bias = own(step_size_bias[0], 0)
    rates = -LOG2E * jnp.exp(own(log_decay_rates[0], 0)).T
    skip = own(mixer_skip_weight[0], 0)

    tokens = input_in_transit[0]
    as_float = tokens.astype(f32)
    square = jnp.sum(as_float * as_float, axis=-1)
    ids = expert_index_table[:, 0].astype(f32)
    small = jnp.concatenate(
        [ids.transpose(0, 2, 1).reshape(2 * STEPS, rows), square[None]], 0
    )
    small = jnp.pad(small, ((0, -small.shape[0] % ROWS), (0, 0)))
    small, present = exchange(
        [small, tokens],
        [(n,) + small.shape, (length, width)],
        [(whole, slot_of), (column_block(width), row_block(rows))],
        "seq",
        1,
    )
    square = small[:, 2 * STEPS].reshape(length)
    all_ids = small[:, : 2 * STEPS].reshape(n, STEPS, 2, rows).transpose(1, 0, 3, 2)
    all_ids = all_ids.reshape(STEPS, length, 2)
    for step in range(STEPS):
        if step:
            as_float = present.astype(f32)
            part = jnp.sum(as_float * as_float, axis=-1).reshape(n, rows)
            part = jnp.pad(part, ((0, -n % ROWS), (0, 0)))
            (part,) = exchange([part], [(n,) + part.shape], [(whole, slot_of)], "seq", 3)
            square = jnp.sum(part, axis=0)[:n].reshape(length)
        scale = lax.rsqrt(square / model + 1e-06)
        normed = (present.astype(f32) * scale[:, None] * gain).astype(bf16)
        padded = jnp.concatenate([jnp.zeros((kernel - 1, width), bf16), normed], 0)
        convolved = conv_bias
        for tap in range(kernel):
            convolved = convolved + taps[tap] * padded[tap : tap + length].astype(f32)
        inner = jax.nn.silu(convolved)
        inner_b = inner.astype(bf16)
        low = jnp.dot(
            inner_b, input_projection[0, :, :rank], preferred_element_type=f32
        ).astype(bf16)
        maps = lax.dot_general(
            input_projection[0, :, rank:],
            inner_b,
            (((0,), (1,)), ((), ())),
            preferred_element_type=f32,
        ).astype(bf16)
        mixed = mix(
            low,
            maps,
            inner,
            present,
            step_size_projection[0],
            dt_bias[None],
            rates,
            skip[None],
            "seq",
            4,
        )
        dispatch, routed = dispatch_of(all_ids[step], n, capacity)
        picked = jnp.dot(dispatch, mixed, preferred_element_type=f32).astype(bf16)
        last = step + 1 == STEPS
        if not last:
            moved = passed_along(mixed, "section")
            moved_ids = passed_along(all_ids[step], "section")
        full = gather(picked, (slots, model), column_block(width), "seq", 6)
        if last:
            mixed = lax.all_to_all(
                mixed.reshape(n, rows, width), "seq", split_axis=0, concat_axis=0
            )
            mixed = mixed.transpose(1, 0, 2).reshape(rows, model)
        full_float = full.astype(f32)
        moe_in = (
            full_float
            * lax.rsqrt(jnp.mean(full_float * full_float, axis=-1, keepdims=True) + 1e-06)
            * expert_norm_gain[0]
        ).astype(bf16)
        logits = jnp.dot(moe_in, router[0], preferred_element_type=f32)
        slot_ids = jnp.dot(dispatch, all_ids[step].astype(bf16), preferred_element_type=f32)
        one_hot = (
            slot_ids[:, :, None] == jnp.arange(experts, dtype=jnp.int32).astype(f32)
        ).astype(f32)
        first = jnp.sum(logits * one_hot[:, 0], axis=1)
        second = jnp.sum(logits * one_hot[:, 1], axis=1)
        weight_one = jax.nn.sigmoid(first - second)
        route = jnp.where(
            slot_ids[:, 0] == 0,
            weight_one,
            jnp.where(slot_ids[:, 1] == 0, 1.0 - weight_one, jnp.zeros_like(weight_one)),
        )
        gate_part = jnp.dot(moe_in, gate_weight[0], preferred_element_type=f32)
        up_part = jnp.dot(moe_in, up_weight[0], preferred_element_type=f32)
        hidden = (jax.nn.silu(gate_part) * up_part).astype(bf16)
        terms = jnp.dot(hidden, down_weight[0], preferred_element_type=f32).astype(bf16)
        if last:
            terms = terms.reshape(n, capacity, model)
            expert_out = scatter_sum(terms, (capacity, model), slot_of, "seq", 8)
            dispatch = lax.dynamic_slice(
                dispatch, (me * capacity, me * rows), (capacity, rows)
            )
            routed = lax.dynamic_slice_in_dim(routed, me * rows, rows, 0)
            route = lax.dynamic_slice_in_dim(route, me * capacity, capacity, 0)
            picked = lax.dynamic_slice_in_dim(full, me * capacity, capacity, 0)
        else:
            expert_out = scatter_sum(terms, (slots, width), column_block(width), "seq", 7)
        expert_out = expert_out.astype(bf16).astype(f32)
        new_rows = (picked.astype(f32) + route[:, None] * expert_out).astype(bf16)
        if not last:
            new_rows = passed_along(new_rows, "section")
            dispatch, routed = dispatch_of(moved_ids, n, capacity)
            mixed = moved
        placed = lax.dot_general(
            dispatch, new_rows, (((0,), (0,)), ((), ())), preferred_element_type=f32
        ).astype(bf16)
        present = jnp.where(routed[:, None], placed, mixed)
    return present[None]


def solution(mesh):
    return jax.shard_map(
        body,
        mesh=mesh,
        in_specs=(
            P("section", "seq", None),
            P("section", None),
            P("section", None, None),
            P("section", None),
            P("section", "seq", None),
            P("section", None, "seq"),
            P("section", None),
            P("section", None, None),
            P("section", None),
            P("section", None),
            P("section", None, None),
            P("section", None, "seq"),
            P("section", None, "seq"),
            P("section", "seq", None),
            P(None, "section", "seq", None),
        ),
        out_specs=P("section", "seq", None),
        check_vma=False,
    )
```

```python
import functools

import jax
import jax.numpy as jnp
from jax import lax
from jax.experimental import pallas as pl
from jax.experimental.pallas import tpu as pltpu
from jax.sharding import PartitionSpec as P

STEPS = 2
LANES = 128
ROWS = 8
LOG2E = 1.4426950408889634
MESH = pl.DeviceIdType.MESH
SMALL_VMEM = 8 * 1024 * 1024
MIX_VMEM = 24 * 1024 * 1024
PIECE = 16
AHEAD = 2
EXPERT_VMEM = 46 * 1024 * 1024


def greet(axis):
    n, me = lax.axis_size(axis), lax.axis_index(axis)
    barrier = pltpu.get_barrier_semaphore()
    for k in range(1, n):
        pl.semaphore_signal(
            barrier, inc=1, device_id={axis: lax.rem(me + k, n)}, device_id_type=MESH
        )
    pl.semaphore_wait(barrier, n - 1)


def exchange_kernel(axis, parts, *refs):
    n, me = lax.axis_size(axis), lax.axis_index(axis)
    count = len(parts)
    send_sem, recv_sem, local_sem = refs[2 * count :]
    greet(axis)
    copies = []
    for k in range(1, n):
        peer = lax.rem(me + k, n)
        for p, (src_at, dst_at) in enumerate(parts):
            copy = pltpu.make_async_remote_copy(
                src_ref=src_at(refs[p], peer),
                dst_ref=dst_at(refs[count + p], me),
                send_sem=send_sem.at[p, k],
                recv_sem=recv_sem.at[p, k],
                device_id={axis: peer},
                device_id_type=MESH,
            )
            copy.start()
            copies.append(copy)
    for p, (src_at, dst_at) in enumerate(parts):
        own = pltpu.make_async_copy(
            src_at(refs[p], me), dst_at(refs[count + p], me), local_sem.at[p]
        )
        own.start()
        copies.append(own)
    for copy in copies:
        copy.wait()


def exchange(xs, shapes, parts, axis, cid):
    n, count = lax.axis_size(axis), len(xs)
    return pl.pallas_call(
        functools.partial(exchange_kernel, axis, parts),
        out_shape=[jax.ShapeDtypeStruct(shape, x.dtype) for x, shape in zip(xs, shapes)],
        in_specs=[pl.BlockSpec(memory_space=pl.ANY)] * count,
        out_specs=[pl.BlockSpec(memory_space=pl.ANY)] * count,
        scratch_shapes=[
            pltpu.SemaphoreType.DMA((count, n)),
            pltpu.SemaphoreType.DMA((count, n)),
            pltpu.SemaphoreType.DMA((count,)),
        ],
        compiler_params=pltpu.CompilerParams(
            collective_id=cid, has_side_effects=True, vmem_limit_bytes=SMALL_VMEM
        ),
        name=f"exchange_{cid}",
    )(*xs)


def spread(axis, block, place, o_ref, send_sem, recv_sem, relay_send, relay_recv, local_sem):
    n, me = lax.axis_size(axis), lax.axis_index(axis)
    partner = me + 1 - 2 * lax.rem(me, 2)

    def send(source, at, target, sent, received):
        copy = pltpu.make_async_remote_copy(
            src_ref=source,
            dst_ref=place(o_ref, at),
            send_sem=sent,
            recv_sem=received,
            device_id={axis: target},
            device_id_type=MESH,
        )
        copy.start()
        return copy

    far = [
        send(block, me, lax.rem(me + 2 * k, n), send_sem.at[k], recv_sem.at[k])
        for k in range(1, n // 2)
    ]
    near = [send(block, me, partner, relay_send.at[0], relay_recv.at[0])]
    own = pltpu.make_async_copy(block, place(o_ref, me), local_sem)
    own.start()
    for k in range(1, n // 2):
        far[k - 1].wait_recv()
        source = lax.rem(me + n - 2 * k, n)
        near.append(
            send(place(o_ref, source), source, partner, relay_send.at[k], relay_recv.at[k])
        )
    for copy in far:
        copy.wait_send()
    for copy in near:
        copy.wait()
    own.wait()


def spread_scratch(n):
    return [pltpu.SemaphoreType.DMA((n // 2,))] * 4 + [pltpu.SemaphoreType.DMA]


def row_block(size):
    return lambda ref, i: ref.at[pl.ds(pl.multiple_of(i * size, size), size), :]


def column_block(size):
    return lambda ref, i: ref.at[:, pl.ds(pl.multiple_of(i * size, size), size)]


def whole(ref, i):
    return ref


def slot_of(ref, i):
    return ref.at[i]


def mixer_kernel(
    axis, nstate, low_ref, maps_ref, x_ref, p_ref, w_ref, bias_ref, a_ref, skip_ref, o_ref,
    full, bc, rs_low, rs_maps, dtb, vb, bb, cx, hb, yb, h_ref, ls, lr, ms, mr, gs, gr, bs, br,
):
    n, me = lax.axis_size(axis), lax.axis_index(axis)
    f32, bf16 = jnp.float32, jnp.bfloat16
    length, width = x_ref.shape
    span = PIECE * n
    blocks = length // span
    groups = nstate // ROWS
    wide = 2 * ROWS * nstate

    def to(peer, source, target, sent, received):
        return pltpu.make_async_remote_copy(
            src_ref=source,
            dst_ref=target,
            send_sem=sent,
            recv_sem=received,
            device_id={axis: peer},
            device_id_type=MESH,
        )

    def rows_of(j, device):
        return pl.ds(pl.multiple_of(j * span + device * PIECE, PIECE), PIECE)

    def lanes_of(j):
        return pl.ds(pl.multiple_of(j * span, span), span)

    def part_low(j, k):
        peer = lax.rem(me + k, n)
        return to(peer, low_ref.at[rows_of(j, peer), :], rs_low.at[j, k], ls.at[j, k], lr.at[j, k])

    def part_maps(j, sender):
        return to(j, maps_ref.at[:, lanes_of(j)], rs_maps.at[sender], ms.at[j], mr.at[sender])

    def sum_low(j, k):
        peer = lax.rem(me + k, n)
        mine = full.at[rows_of(j, me), :]
        return to(peer, mine, mine, gs.at[j, k], gr.at[j, k])

    def sum_maps(j, k):
        mine = bc.at[:, lanes_of(j)]
        return to(lax.rem(me + k, n), mine, mine, bs.at[k], br.at[j])

    def send_parts(j):
        @pl.when(me != j)
        def _():
            part_maps(j, me).start()

        for k in range(1, n):
            part_low(j, k).start()

    def reduce_and_send(j):
        total = low_ref[rows_of(j, me), :].astype(f32)
        for k in range(1, n):
            part_low(j, k).wait_recv()
            total = total + rs_low[j, k].astype(f32)
        full[rows_of(j, me), :] = total.astype(bf16)
        for k in range(1, n):
            sum_low(j, k).start()

        @pl.when(me == j)
        def _():
            maps = maps_ref[:, lanes_of(j)].astype(f32)
            for k in range(1, n):
                sender = lax.rem(me + k, n)
                part_maps(j, sender).wait_recv()
                maps = maps + rs_maps[sender].astype(f32)
            high = maps.astype(bf16)
            bc[: 2 * nstate, lanes_of(j)] = high
            bc[2 * nstate :, lanes_of(j)] = (maps - high.astype(f32)).astype(bf16)
            for k in range(1, n):
                sum_maps(j, k).start()

    spread_map = (
        lax.broadcasted_iota(jnp.int32, (nstate, wide), 1) % nstate
        == lax.broadcasted_iota(jnp.int32, (nstate, wide), 0)
    ).astype(bf16)
    own = (
        lax.broadcasted_iota(jnp.int32, (LANES, wide), 1) // nstate
        == lax.broadcasted_iota(jnp.int32, (LANES, wide), 0) % (2 * ROWS)
    )

    def chunk(start):
        here = pl.ds(pl.multiple_of(start, LANES), LANES)
        z = jnp.dot(full[here, :], w_ref[...], preferred_element_type=f32) + bias_ref[...]
        step = jnp.maximum(z, 0.0) + jnp.log1p(jnp.exp(-jnp.abs(z)))
        dtb[...] = step
        vb[...] = step * x_ref[here, :]
        maps = bc[: 2 * nstate, here].astype(f32) + bc[2 * nstate :, here].astype(f32)
        for k in range(LANES):
            bb[k * nstate : (k + 1) * nstate, :] = jnp.broadcast_to(
                maps[:nstate, k : k + 1], (nstate, LANES)
            )
        c = maps[nstate:]
        c_hi = c.astype(bf16)
        c_lo = (c - c_hi.astype(f32)).astype(bf16)
        for i, part in enumerate((c_hi, c_lo)):
            placed = lax.dot_general(
                part, spread_map, (((0,), (0,)), ((), ())), preferred_element_type=f32
            )
            cx[i] = jnp.where(own, placed, 0.0)
        rates = [a_ref[g * ROWS : (g + 1) * ROWS, :] for g in range(groups)]

        def tokens(i, states):
            states = list(states)
            base = pl.multiple_of(i * ROWS, ROWS)
            for k in range(ROWS):
                d = jnp.broadcast_to(dtb[pl.ds(base + k, 1), :], (ROWS, width))
                v = jnp.broadcast_to(vb[pl.ds(base + k, 1), :], (ROWS, width))
                row = pl.multiple_of((base + k) * nstate, nstate)
                for g in range(groups):
                    b = jnp.tile(bb[pl.ds(row + g * ROWS, ROWS), :], (1, width // LANES))
                    states[g] = jnp.exp2(d * rates[g]) * states[g] + v * b
                hb[pl.ds(row, nstate), :] = jnp.concatenate(states, 0).astype(bf16)
            return tuple(states)

        states = tuple(h_ref[g * ROWS : (g + 1) * ROWS, :] for g in range(groups))
        states = lax.fori_loop(0, LANES // ROWS, tokens, states)
        for g in range(groups):
            h_ref[g * ROWS : (g + 1) * ROWS, :] = states[g]
        for i in range(LANES // (2 * ROWS)):
            at = slice(i * 2 * ROWS, (i + 1) * 2 * ROWS)
            left = jnp.concatenate([cx[0, at, :], cx[1, at, :]], 0).astype(bf16)
            y = jnp.dot(left, hb[i * wide : (i + 1) * wide, :], preferred_element_type=f32)
            yb[at, :] = y[: 2 * ROWS] + y[2 * ROWS :]
        o_ref[here, :] = (
            p_ref[here, :].astype(f32) + (yb[...] + skip_ref[...] * x_ref[here, :])
        ).astype(bf16)

    h_ref[...] = jnp.zeros_like(h_ref)
    greet(axis)
    for j in range(AHEAD + 1):
        send_parts(j)
    for j in range(AHEAD):
        reduce_and_send(j)

    def block(j, carry):
        @pl.when(j + AHEAD + 1 < blocks)
        def _():
            send_parts(j + AHEAD + 1)

        @pl.when(j + AHEAD < blocks)
        def _():
            reduce_and_send(j + AHEAD)

        for k in range(1, n):
            sum_low(j, k).wait_recv()

        @pl.when(me != j)
        def _():
            sum_maps(j, 1).wait_recv()

        for i in range(span // LANES):
            chunk(j * span + i * LANES)
        return carry

    lax.fori_loop(0, blocks, block, 0)

    def finish(j, carry):
        @pl.when(me != j)
        def _():
            part_maps(j, me).wait_send()

        for k in range(1, n):
            part_low(j, k).wait_send()
            sum_low(j, k).wait_send()
        return carry

    lax.fori_loop(0, blocks, finish, 0)

    @pl.when(me < blocks)
    def _():
        for k in range(1, n):
            sum_maps(me, k).wait_send()


def mix(low, maps, x, present, w, bias, rates, skip, axis, cid):
    n = lax.axis_size(axis)
    length, width = x.shape
    nstate, rank = rates.shape[0], w.shape[0]
    span = PIECE * n
    blocks = length // span
    wide = 2 * ROWS * nstate
    f32, bf16 = jnp.float32, jnp.bfloat16
    dma = pltpu.SemaphoreType.DMA
    return pl.pallas_call(
        functools.partial(mixer_kernel, axis, nstate),
        out_shape=jax.ShapeDtypeStruct((length, width), bf16),
        in_specs=[pl.BlockSpec(memory_space=pltpu.VMEM)] * 8,
        out_specs=pl.BlockSpec(memory_space=pltpu.VMEM),
        scratch_shapes=[
            pltpu.VMEM((length, rank), bf16),
            pltpu.VMEM((4 * nstate, length), bf16),
            pltpu.VMEM((blocks, n, PIECE, rank), bf16),
            pltpu.VMEM((n, 2 * nstate, span), bf16),
            pltpu.VMEM((LANES, width), f32),
            pltpu.VMEM((LANES, width), f32),
            pltpu.VMEM((LANES * nstate, LANES), f32),
            pltpu.VMEM((2, LANES, wide), f32),
            pltpu.VMEM((LANES * nstate, width), bf16),
            pltpu.VMEM((LANES, width), f32),
            pltpu.VMEM((nstate, width), f32),
            dma((blocks, n)),
            dma((blocks, n)),
            dma((blocks,)),
            dma((n,)),
            dma((blocks, n)),
            dma((blocks, n)),
            dma((n,)),
            dma((blocks,)),
        ],
        compiler_params=pltpu.CompilerParams(
            collective_id=cid, has_side_effects=True, vmem_limit_bytes=MIX_VMEM
        ),
        cost_estimate=pl.CostEstimate(
            flops=6 * length * width * nstate,
            bytes_accessed=12 * length * width,
            transcendentals=length * width * nstate,
        ),
        name=f"mix_{cid}",
    )(low, maps, x, present, w, bias, rates, skip)


def expert_kernel(
    axis, last, columns, picked_ref, gain_ref, router_ref, choice_ref, marks_ref, gate_hbm, up_hbm, down_hbm,
    *refs,
):
    n, me = lax.axis_size(axis), lax.axis_index(axis)
    f32, bf16 = jnp.float32, jnp.bfloat16
    slots, width = picked_ref.shape
    model, ff = gate_hbm.shape
    pieces = ff // columns
    if last:
        o_ref, route_ref, full = refs[:3]
        refs = refs[3:]
    else:
        o_ref, full = refs[:2]
        refs = refs[2:]
    moe_in, hidden, gate, up, down, terms, held = refs[:7]
    gate_sem, up_sem, down_sem, out_sem, in_sem = refs[7:12]
    sems = refs[12:]

    def fetch_in(hbm, buf, sem, i):
        at = pl.ds(pl.multiple_of(i * columns, columns), columns)
        return pltpu.make_async_copy(hbm.at[:, at], buf.at[i], sem.at[i])

    def fetch_down(k):
        block = k if last else lax.rem(me + k, n)
        at = pl.ds(pl.multiple_of(block * width, width), width)
        return pltpu.make_async_copy(down_hbm.at[:, at], down.at[k], down_sem.at[k])

    for i in range(pieces):
        fetch_in(gate_hbm, gate, gate_sem, i).start()
        fetch_in(up_hbm, up, up_sem, i).start()
    for k in range(n):
        fetch_down(k if last else (k + 1) % n).start()

    greet(axis)
    spread(axis, picked_ref, column_block(width), full, *sems)

    square = jnp.zeros((slots, 1), f32)
    for i in range(0, model, columns):
        part = full[:, i : i + columns].astype(f32)
        square = square + jnp.sum(part * part, axis=1, keepdims=True)
    scale = lax.rsqrt(square / model + 1e-06)
    for i in range(0, model, columns):
        at = slice(i, i + columns)
        moe_in[:, at] = (full[:, at].astype(f32) * scale * gain_ref[:, at]).astype(bf16)

    def piece(i, carry):
        fetch_in(gate_hbm, gate, gate_sem, i).wait()
        gate_part = jnp.dot(moe_in[...], gate[i], preferred_element_type=f32)
        fetch_in(up_hbm, up, up_sem, i).wait()
        up_part = jnp.dot(moe_in[...], up[i], preferred_element_type=f32)
        at = pl.ds(pl.multiple_of(i * columns, columns), columns)
        hidden[:, at] = (gate_part * jax.nn.sigmoid(gate_part) * up_part).astype(bf16)
        return carry

    lax.fori_loop(0, pieces, piece, 0)

    def term(k):
        fetch_down(k).wait()
        return jnp.dot(hidden[...], down[k], preferred_element_type=f32)

    def to(peer, source, target, i, k):
        return pltpu.make_async_remote_copy(
            src_ref=source,
            dst_ref=target,
            send_sem=out_sem.at[i, k],
            recv_sem=in_sem.at[i, k],
            device_id={axis: peer},
            device_id_type=MESH,
        )

    half = model // 2

    def part_of(k, i):
        peer = lax.rem(me + k, n)
        if not last:
            return to(peer, terms.at[k], held.at[k], 0, k)
        at = pl.ds(i * half, half)
        return to(peer, terms.at[peer, :, at], held.at[k, :, at], i, k)

    def route():
        logits = lax.dot_general(
            moe_in[...], router_ref[...], (((1,), (1,)), ((), ())), preferred_element_type=f32
        )
        one = jax.nn.sigmoid(jnp.sum(logits * choice_ref[...], axis=1, keepdims=True))
        marks = marks_ref[...]
        return marks[:, 0:1] * one + marks[:, 1:2] * (1.0 - one)

    if last:
        capacity = slots // n

        def rows(q, carry):
            at = pl.ds(pl.multiple_of(q * width, width), width)
            terms[:, :, at] = term(q).reshape(n, capacity, width).astype(bf16)
            return carry

        for i in range(2):
            lax.fori_loop(i * n // 2, (i + 1) * n // 2, rows, 0)
            for k in range(1, n):
                part_of(k, i).start()
        route_ref[...] = route()
        total = terms[me].astype(f32)
        for k in range(1, n):
            for i in range(2):
                part_of(k, i).wait()
            total = total + held[k].astype(f32)
        o_ref[...] = total.astype(bf16)
    else:

        def block(k, carry):
            terms[k] = term(k).astype(bf16)
            part_of(k, 0).start()
            return carry

        lax.fori_loop(1, n, block, 0)
        total = term(0).astype(bf16).astype(f32)
        weight = route()
        for k in range(1, n):
            part_of(k, 0).wait()
            total = total + held[k].astype(f32)
        expert_out = total.astype(bf16).astype(f32)
        o_ref[...] = (picked_ref[...].astype(f32) + weight * expert_out).astype(bf16)


def expert(picked, gain, router, choice, marks, gate, up, down, last, axis, cid):
    n = lax.axis_size(axis)
    slots, width = picked.shape
    model, ff = gate.shape
    columns = 512 if ff % 512 == 0 else ff
    f32, bf16 = jnp.float32, jnp.bfloat16
    dma = pltpu.SemaphoreType.DMA
    vmem = pl.BlockSpec(memory_space=pltpu.VMEM)
    hbm = pl.BlockSpec(memory_space=pltpu.HBM)
    part = (slots // n, model) if last else (slots, width)
    rows = jax.ShapeDtypeStruct(part, bf16)
    full = jax.ShapeDtypeStruct((slots, model), bf16)
    if last:
        out_shape = [rows, jax.ShapeDtypeStruct((slots, 1), f32), full]
    else:
        out_shape = [rows, full]
    return pl.pallas_call(
        functools.partial(expert_kernel, axis, last, columns),
        out_shape=out_shape,
        in_specs=[vmem] * 5 + [hbm] * 3,
        out_specs=[vmem] * len(out_shape),
        scratch_shapes=[
            pltpu.VMEM((slots, model), bf16),
            pltpu.VMEM((slots, ff), bf16),
            pltpu.VMEM((ff // columns, model, columns), bf16),
            pltpu.VMEM((ff // columns, model, columns), bf16),
            pltpu.VMEM((n, ff, width), bf16),
            pltpu.VMEM((n,) + part, bf16),
            pltpu.VMEM((n,) + part, bf16),
            dma((ff // columns,)),
            dma((ff // columns,)),
            dma((n,)),
            dma((2, n)),
            dma((2, n)),
        ]
        + spread_scratch(n),
        compiler_params=pltpu.CompilerParams(
            collective_id=cid, has_side_effects=True, vmem_limit_bytes=EXPERT_VMEM
        ),
        cost_estimate=pl.CostEstimate(
            flops=6 * slots * model * ff,
            bytes_accessed=6 * model * ff,
            transcendentals=slots * ff,
        ),
        name=f"expert_{cid}",
    )(picked, gain, router, choice, marks, gate, up, down)


def passed_along(x, axis):
    length = lax.axis_size(axis)
    return lax.ppermute(x, axis, [(i, (i + 1) % length) for i in range(length)])


def dispatch_of(ids, blocks, capacity):
    length = ids.shape[0]
    size = length // blocks
    routed = (ids[:, 0] == 0) | (ids[:, 1] == 0)
    counted = routed.astype(jnp.float32).reshape(blocks, size)
    before = jnp.tril(jnp.ones((size, size), jnp.float32), -1)
    rank = jnp.dot(counted, before.T).reshape(length)
    slot = rank.astype(jnp.int32) + (jnp.arange(length, dtype=jnp.int32) // size) * capacity
    chosen = (jnp.arange(blocks * capacity, dtype=jnp.int32)[:, None] == slot[None, :]) & routed[
        None, :
    ]
    return chosen.astype(jnp.bfloat16), routed


def body(
    input_in_transit,
    mixer_norm_gain,
    convolution_weight,
    convolution_bias,
    input_projection,
    step_size_projection,
    step_size_bias,
    log_decay_rates,
    mixer_skip_weight,
    expert_norm_gain,
    router,
    gate_weight,
    up_weight,
    down_weight,
    expert_index_table,
):
    n, me = lax.axis_size("seq"), lax.axis_index("seq")
    experts = router.shape[2]
    rows = input_in_transit.shape[1]
    model = input_in_transit.shape[2]
    nstate = log_decay_rates.shape[2]
    rank = step_size_projection.shape[1]
    kernel = convolution_weight.shape[1]
    capacity = rows // 16
    length, width = rows * n, model // n
    slots = capacity * n
    f32, bf16 = jnp.float32, jnp.bfloat16

    def own(weight, axis):
        return lax.dynamic_slice_in_dim(weight, me * width, width, axis)

    gain = own(mixer_norm_gain[0], 0)
    taps = own(convolution_weight[0], 1)
    conv_bias = own(convolution_bias[0], 0)
    dt_bias = own(step_size_bias[0], 0)
    rates = -LOG2E * jnp.exp(own(log_decay_rates[0], 0)).T
    skip = own(mixer_skip_weight[0], 0)

    tokens = input_in_transit[0]
    as_float = tokens.astype(f32)
    square = jnp.sum(as_float * as_float, axis=-1)
    ids = expert_index_table[:, 0].astype(f32)
    small = jnp.concatenate(
        [ids.transpose(0, 2, 1).reshape(2 * STEPS, rows), square[None]], 0
    )
    small = jnp.pad(small, ((0, -small.shape[0] % ROWS), (0, 0)))
    small, present = exchange(
        [small, tokens],
        [(n,) + small.shape, (length, width)],
        [(whole, slot_of), (column_block(width), row_block(rows))],
        "seq",
        1,
    )
    square = small[:, 2 * STEPS].reshape(length)
    all_ids = small[:, : 2 * STEPS].reshape(n, STEPS, 2, rows).transpose(1, 0, 3, 2)
    all_ids = all_ids.reshape(STEPS, length, 2)
    for step in range(STEPS):
        if step:
            as_float = present.astype(f32)
            part = jnp.sum(as_float * as_float, axis=-1).reshape(n, rows)
            part = jnp.pad(part, ((0, -n % ROWS), (0, 0)))
            (part,) = exchange([part], [(n,) + part.shape], [(whole, slot_of)], "seq", 3)
            square = jnp.sum(part, axis=0)[:n].reshape(length)
        scale = lax.rsqrt(square / model + 1e-06)
        normed = (present.astype(f32) * scale[:, None] * gain).astype(bf16)
        padded = jnp.concatenate([jnp.zeros((kernel - 1, width), bf16), normed], 0)
        convolved = conv_bias
        for tap in range(kernel):
            convolved = convolved + taps[tap] * padded[tap : tap + length].astype(f32)
        inner = jax.nn.silu(convolved)
        inner_b = inner.astype(bf16)
        low = jnp.dot(
            inner_b, input_projection[0, :, :rank], preferred_element_type=f32
        ).astype(bf16)
        maps = lax.dot_general(
            input_projection[0, :, rank:],
            inner_b,
            (((0,), (1,)), ((), ())),
            preferred_element_type=f32,
        ).astype(bf16)
        mixed = mix(
            low,
            maps,
            inner,
            present,
            step_size_projection[0],
            dt_bias[None],
            rates,
            skip[None],
            "seq",
            4,
        )
        dispatch, routed = dispatch_of(all_ids[step], n, capacity)
        picked = jnp.dot(dispatch, mixed, preferred_element_type=f32).astype(bf16)
        last = step + 1 == STEPS
        if not last:
            moved = passed_along(mixed, "section")
            moved_ids = passed_along(all_ids[step], "section")
        if last:
            mixed = lax.all_to_all(
                mixed.reshape(n, rows, width), "seq", split_axis=0, concat_axis=0
            )
            mixed = mixed.transpose(1, 0, 2).reshape(rows, model)
        slot_ids = jnp.dot(dispatch, all_ids[step].astype(bf16), preferred_element_type=f32)
        one_hot = (
            slot_ids[:, :, None] == jnp.arange(experts, dtype=jnp.int32).astype(f32)
        ).astype(f32)
        choice = one_hot[:, 0] - one_hot[:, 1]
        is_first = slot_ids[:, 0] == 0
        is_second = (slot_ids[:, 1] == 0) & ~is_first
        marks = jnp.stack([is_first, is_second], 1).astype(f32)
        outs = expert(
            picked,
            expert_norm_gain,
            router[0].T,
            choice,
            marks,
            gate_weight[0],
            up_weight[0],
            down_weight[0],
            last,
            "seq",
            8 if last else 7,
        )
        if last:
            expert_out, route, full = outs
            dispatch = lax.dynamic_slice(
                dispatch, (me * capacity, me * rows), (capacity, rows)
            )
            routed = lax.dynamic_slice_in_dim(routed, me * rows, rows, 0)
            route = lax.dynamic_slice_in_dim(route, me * capacity, capacity, 0)
            picked = lax.dynamic_slice_in_dim(full, me * capacity, capacity, 0)
            new_rows = (picked.astype(f32) + route * expert_out.astype(f32)).astype(bf16)
        else:
            new_rows = passed_along(outs[0], "section")
            dispatch, routed = dispatch_of(moved_ids, n, capacity)
            mixed = moved
        placed = lax.dot_general(
            dispatch, new_rows, (((0,), (0,)), ((), ())), preferred_element_type=f32
        ).astype(bf16)
        present = jnp.where(routed[:, None], placed, mixed)
    return present[None]


def solution(mesh):
    return jax.shard_map(
        body,
        mesh=mesh,
        in_specs=(
            P("section", "seq", None),
            P("section", None),
            P("section", None, None),
            P("section", None),
            P("section", "seq", None),
            P("section", None, "seq"),
            P("section", None),
            P("section", None, None),
            P("section", None),
            P("section", None),
            P("section", None, None),
            P("section", None, "seq"),
            P("section", None, "seq"),
            P("section", "seq", None),
            P(None, "section", "seq", None),
        ),
        out_specs=P("section", "seq", None),
        check_vma=False,
    )
```

```python
import functools

import jax
import jax.numpy as jnp
from jax import lax
from jax.experimental import pallas as pl
from jax.experimental.pallas import tpu as pltpu
from jax.sharding import PartitionSpec as P

STEPS = 2
LANES = 128
ROWS = 8
LOG2E = 1.4426950408889634
MESH = pl.DeviceIdType.MESH
SMALL_VMEM = 8 * 1024 * 1024
MIX_VMEM = 24 * 1024 * 1024
PIECE = 16
AHEAD = 2
EXPERT_VMEM = 50 * 1024 * 1024


def greet(axis, ring=None):
    n, me = lax.axis_size(axis), lax.axis_index(axis)
    barrier = pltpu.get_barrier_semaphore()
    for k in range(1, n):
        pl.semaphore_signal(
            barrier, inc=1, device_id={axis: lax.rem(me + k, n)}, device_id_type=MESH
        )
    count = n - 1
    if ring is not None:
        size, at = lax.axis_size(ring), lax.axis_index(ring)
        for k in (1, size - 1):
            pl.semaphore_signal(
                barrier, inc=1, device_id={ring: lax.rem(at + k, size)}, device_id_type=MESH
            )
        count = count + 2
    pl.semaphore_wait(barrier, count)


def exchange_kernel(axis, parts, *refs):
    n, me = lax.axis_size(axis), lax.axis_index(axis)
    count = len(parts)
    send_sem, recv_sem, local_sem = refs[2 * count :]
    greet(axis)
    copies = []
    for k in range(1, n):
        peer = lax.rem(me + k, n)
        for p, (src_at, dst_at) in enumerate(parts):
            copy = pltpu.make_async_remote_copy(
                src_ref=src_at(refs[p], peer),
                dst_ref=dst_at(refs[count + p], me),
                send_sem=send_sem.at[p, k],
                recv_sem=recv_sem.at[p, k],
                device_id={axis: peer},
                device_id_type=MESH,
            )
            copy.start()
            copies.append(copy)
    for p, (src_at, dst_at) in enumerate(parts):
        own = pltpu.make_async_copy(
            src_at(refs[p], me), dst_at(refs[count + p], me), local_sem.at[p]
        )
        own.start()
        copies.append(own)
    for copy in copies:
        copy.wait()


def exchange(xs, shapes, parts, axis, cid):
    n, count = lax.axis_size(axis), len(xs)
    return pl.pallas_call(
        functools.partial(exchange_kernel, axis, parts),
        out_shape=[jax.ShapeDtypeStruct(shape, x.dtype) for x, shape in zip(xs, shapes)],
        in_specs=[pl.BlockSpec(memory_space=pl.ANY)] * count,
        out_specs=[pl.BlockSpec(memory_space=pl.ANY)] * count,
        scratch_shapes=[
            pltpu.SemaphoreType.DMA((count, n)),
            pltpu.SemaphoreType.DMA((count, n)),
            pltpu.SemaphoreType.DMA((count,)),
        ],
        compiler_params=pltpu.CompilerParams(
            collective_id=cid, has_side_effects=True, vmem_limit_bytes=SMALL_VMEM
        ),
        name=f"exchange_{cid}",
    )(*xs)


def spread(axis, block, place, o_ref, send_sem, recv_sem, relay_send, relay_recv, local_sem):
    n, me = lax.axis_size(axis), lax.axis_index(axis)
    partner = me + 1 - 2 * lax.rem(me, 2)

    def send(source, at, target, sent, received):
        copy = pltpu.make_async_remote_copy(
            src_ref=source,
            dst_ref=place(o_ref, at),
            send_sem=sent,
            recv_sem=received,
            device_id={axis: target},
            device_id_type=MESH,
        )
        copy.start()
        return copy

    far = [
        send(block, me, lax.rem(me + 2 * k, n), send_sem.at[k], recv_sem.at[k])
        for k in range(1, n // 2)
    ]
    near = [send(block, me, partner, relay_send.at[0], relay_recv.at[0])]
    own = pltpu.make_async_copy(block, place(o_ref, me), local_sem)
    own.start()
    for k in range(1, n // 2):
        far[k - 1].wait_recv()
        source = lax.rem(me + n - 2 * k, n)
        near.append(
            send(place(o_ref, source), source, partner, relay_send.at[k], relay_recv.at[k])
        )
    for copy in far:
        copy.wait_send()
    for copy in near:
        copy.wait()
    own.wait()


def spread_scratch(n):
    return [pltpu.SemaphoreType.DMA((n // 2,))] * 4 + [pltpu.SemaphoreType.DMA]


def row_block(size):
    return lambda ref, i: ref.at[pl.ds(pl.multiple_of(i * size, size), size), :]


def column_block(size):
    return lambda ref, i: ref.at[:, pl.ds(pl.multiple_of(i * size, size), size)]


def whole(ref, i):
    return ref


def slot_of(ref, i):
    return ref.at[i]


def mixer_kernel(
    axis, nstate, low_ref, maps_ref, x_ref, p_ref, w_ref, bias_ref, a_ref, skip_ref, o_ref,
    full, bc, rs_low, rs_maps, dtb, vb, bb, cx, hb, yb, h_ref, ls, lr, ms, mr, gs, gr, bs, br,
):
    n, me = lax.axis_size(axis), lax.axis_index(axis)
    f32, bf16 = jnp.float32, jnp.bfloat16
    length, width = x_ref.shape
    span = PIECE * n
    blocks = length // span
    groups = nstate // ROWS
    wide = 2 * ROWS * nstate

    def to(peer, source, target, sent, received):
        return pltpu.make_async_remote_copy(
            src_ref=source,
            dst_ref=target,
            send_sem=sent,
            recv_sem=received,
            device_id={axis: peer},
            device_id_type=MESH,
        )

    def rows_of(j, device):
        return pl.ds(pl.multiple_of(j * span + device * PIECE, PIECE), PIECE)

    def lanes_of(j):
        return pl.ds(pl.multiple_of(j * span, span), span)

    def part_low(j, k):
        peer = lax.rem(me + k, n)
        return to(peer, low_ref.at[rows_of(j, peer), :], rs_low.at[j, k], ls.at[j, k], lr.at[j, k])

    def part_maps(j, sender):
        return to(j, maps_ref.at[:, lanes_of(j)], rs_maps.at[sender], ms.at[j], mr.at[sender])

    def sum_low(j, k):
        peer = lax.rem(me + k, n)
        mine = full.at[rows_of(j, me), :]
        return to(peer, mine, mine, gs.at[j, k], gr.at[j, k])

    def sum_maps(j, k):
        mine = bc.at[:, lanes_of(j)]
        return to(lax.rem(me + k, n), mine, mine, bs.at[k], br.at[j])

    def send_parts(j):
        @pl.when(me != j)
        def _():
            part_maps(j, me).start()

        for k in range(1, n):
            part_low(j, k).start()

    def reduce_and_send(j):
        total = low_ref[rows_of(j, me), :].astype(f32)
        for k in range(1, n):
            part_low(j, k).wait_recv()
            total = total + rs_low[j, k].astype(f32)
        full[rows_of(j, me), :] = total.astype(bf16)
        for k in range(1, n):
            sum_low(j, k).start()

        @pl.when(me == j)
        def _():
            maps = maps_ref[:, lanes_of(j)].astype(f32)
            for k in range(1, n):
                sender = lax.rem(me + k, n)
                part_maps(j, sender).wait_recv()
                maps = maps + rs_maps[sender].astype(f32)
            high = maps.astype(bf16)
            bc[: 2 * nstate, lanes_of(j)] = high
            bc[2 * nstate :, lanes_of(j)] = (maps - high.astype(f32)).astype(bf16)
            for k in range(1, n):
                sum_maps(j, k).start()

    spread_map = (
        lax.broadcasted_iota(jnp.int32, (nstate, wide), 1) % nstate
        == lax.broadcasted_iota(jnp.int32, (nstate, wide), 0)
    ).astype(bf16)
    own = (
        lax.broadcasted_iota(jnp.int32, (LANES, wide), 1) // nstate
        == lax.broadcasted_iota(jnp.int32, (LANES, wide), 0) % (2 * ROWS)
    )

    def chunk(start):
        here = pl.ds(pl.multiple_of(start, LANES), LANES)
        z = jnp.dot(full[here, :], w_ref[...], preferred_element_type=f32) + bias_ref[...]
        step = jnp.maximum(z, 0.0) + jnp.log1p(jnp.exp(-jnp.abs(z)))
        dtb[...] = step
        vb[...] = step * x_ref[here, :]
        maps = bc[: 2 * nstate, here].astype(f32) + bc[2 * nstate :, here].astype(f32)
        for k in range(LANES):
            bb[k * nstate : (k + 1) * nstate, :] = jnp.broadcast_to(
                maps[:nstate, k : k + 1], (nstate, LANES)
            )
        c = maps[nstate:]
        c_hi = c.astype(bf16)
        c_lo = (c - c_hi.astype(f32)).astype(bf16)
        for i, part in enumerate((c_hi, c_lo)):
            placed = lax.dot_general(
                part, spread_map, (((0,), (0,)), ((), ())), preferred_element_type=f32
            )
            cx[i] = jnp.where(own, placed, 0.0)
        rates = [a_ref[g * ROWS : (g + 1) * ROWS, :] for g in range(groups)]

        def tokens(i, states):
            states = list(states)
            base = pl.multiple_of(i * ROWS, ROWS)
            for k in range(ROWS):
                d = jnp.broadcast_to(dtb[pl.ds(base + k, 1), :], (ROWS, width))
                v = jnp.broadcast_to(vb[pl.ds(base + k, 1), :], (ROWS, width))
                row = pl.multiple_of((base + k) * nstate, nstate)
                for g in range(groups):
                    b = jnp.tile(bb[pl.ds(row + g * ROWS, ROWS), :], (1, width // LANES))
                    states[g] = jnp.exp2(d * rates[g]) * states[g] + v * b
                hb[pl.ds(row, nstate), :] = jnp.concatenate(states, 0).astype(bf16)
            return tuple(states)

        states = tuple(h_ref[g * ROWS : (g + 1) * ROWS, :] for g in range(groups))
        states = lax.fori_loop(0, LANES // ROWS, tokens, states)
        for g in range(groups):
            h_ref[g * ROWS : (g + 1) * ROWS, :] = states[g]
        for i in range(LANES // (2 * ROWS)):
            at = slice(i * 2 * ROWS, (i + 1) * 2 * ROWS)
            left = jnp.concatenate([cx[0, at, :], cx[1, at, :]], 0).astype(bf16)
            y = jnp.dot(left, hb[i * wide : (i + 1) * wide, :], preferred_element_type=f32)
            yb[at, :] = y[: 2 * ROWS] + y[2 * ROWS :]
        o_ref[here, :] = (
            p_ref[here, :].astype(f32) + (yb[...] + skip_ref[...] * x_ref[here, :])
        ).astype(bf16)

    h_ref[...] = jnp.zeros_like(h_ref)
    greet(axis)
    for j in range(AHEAD + 1):
        send_parts(j)
    for j in range(AHEAD):
        reduce_and_send(j)

    def block(j, carry):
        @pl.when(j + AHEAD + 1 < blocks)
        def _():
            send_parts(j + AHEAD + 1)

        @pl.when(j + AHEAD < blocks)
        def _():
            reduce_and_send(j + AHEAD)

        for k in range(1, n):
            sum_low(j, k).wait_recv()

        @pl.when(me != j)
        def _():
            sum_maps(j, 1).wait_recv()

        for i in range(span // LANES):
            chunk(j * span + i * LANES)
        return carry

    lax.fori_loop(0, blocks, block, 0)

    def finish(j, carry):
        @pl.when(me != j)
        def _():
            part_maps(j, me).wait_send()

        for k in range(1, n):
            part_low(j, k).wait_send()
            sum_low(j, k).wait_send()
        return carry

    lax.fori_loop(0, blocks, finish, 0)

    @pl.when(me < blocks)
    def _():
        for k in range(1, n):
            sum_maps(me, k).wait_send()


def mix(low, maps, x, present, w, bias, rates, skip, axis, cid):
    n = lax.axis_size(axis)
    length, width = x.shape
    nstate, rank = rates.shape[0], w.shape[0]
    span = PIECE * n
    blocks = length // span
    wide = 2 * ROWS * nstate
    f32, bf16 = jnp.float32, jnp.bfloat16
    dma = pltpu.SemaphoreType.DMA
    return pl.pallas_call(
        functools.partial(mixer_kernel, axis, nstate),
        out_shape=jax.ShapeDtypeStruct((length, width), bf16),
        in_specs=[pl.BlockSpec(memory_space=pltpu.VMEM)] * 8,
        out_specs=pl.BlockSpec(memory_space=pltpu.VMEM),
        scratch_shapes=[
            pltpu.VMEM((length, rank), bf16),
            pltpu.VMEM((4 * nstate, length), bf16),
            pltpu.VMEM((blocks, n, PIECE, rank), bf16),
            pltpu.VMEM((n, 2 * nstate, span), bf16),
            pltpu.VMEM((LANES, width), f32),
            pltpu.VMEM((LANES, width), f32),
            pltpu.VMEM((LANES * nstate, LANES), f32),
            pltpu.VMEM((2, LANES, wide), f32),
            pltpu.VMEM((LANES * nstate, width), bf16),
            pltpu.VMEM((LANES, width), f32),
            pltpu.VMEM((nstate, width), f32),
            dma((blocks, n)),
            dma((blocks, n)),
            dma((blocks,)),
            dma((n,)),
            dma((blocks, n)),
            dma((blocks, n)),
            dma((n,)),
            dma((blocks,)),
        ],
        compiler_params=pltpu.CompilerParams(
            collective_id=cid, has_side_effects=True, vmem_limit_bytes=MIX_VMEM
        ),
        cost_estimate=pl.CostEstimate(
            flops=6 * length * width * nstate,
            bytes_accessed=12 * length * width,
            transcendentals=length * width * nstate,
        ),
        name=f"mix_{cid}",
    )(low, maps, x, present, w, bias, rates, skip)


def expert_kernel(
    axis, ring, last, columns, picked_ref, gain_ref, router_ref, choice_ref, marks_ref, extra_ref, gate_hbm, up_hbm,
    down_hbm,
    *refs,
):
    n, me = lax.axis_size(axis), lax.axis_index(axis)
    f32, bf16 = jnp.float32, jnp.bfloat16
    slots, width = picked_ref.shape
    model, ff = gate_hbm.shape
    pieces = ff // columns
    if last:
        o_ref, route_ref, full, moved = refs[:4]
    else:
        o_ref, full, arrived, arrived_ids = refs[:4]
    refs = refs[4:]
    moe_in, hidden, gate, up, down, terms, held = refs[:7]
    gate_sem, up_sem, down_sem, out_sem, in_sem, far_out, far_in, own_sem = refs[7:15]
    sems = refs[15:]

    def fetch_in(hbm, buf, sem, i):
        at = pl.ds(pl.multiple_of(i * columns, columns), columns)
        return pltpu.make_async_copy(hbm.at[:, at], buf.at[i], sem.at[i])

    def fetch_down(k):
        block = k if last else lax.rem(me + k, n)
        at = pl.ds(pl.multiple_of(block * width, width), width)
        return pltpu.make_async_copy(down_hbm.at[:, at], down.at[k], down_sem.at[k])

    for i in range(pieces):
        fetch_in(gate_hbm, gate, gate_sem, i).start()
        fetch_in(up_hbm, up, up_sem, i).start()
    for k in range(n):
        fetch_down(k if last else (k + 1) % n).start()

    def far(device, source, target, k):
        return pltpu.make_async_remote_copy(
            src_ref=source,
            dst_ref=target,
            send_sem=far_out.at[k],
            recv_sem=far_in.at[k],
            device_id=device,
            device_id_type=MESH,
        )

    sent = []
    if last:
        greet(axis)
        spread(axis, picked_ref, column_block(width), full, *sems)
        mine = column_block(width)(moved, me)
        block_of = row_block(extra_ref.shape[0] // n)
        for k in range(1, n):
            peer = lax.rem(me + k, n)
            sent.append(far({axis: peer}, block_of(extra_ref, peer), mine, k))
        sent.append(pltpu.make_async_copy(block_of(extra_ref, me), mine, own_sem))
        for copy in sent:
            copy.start()
    else:
        greet(axis, ring)
        size = lax.axis_size(ring)
        following = {ring: lax.rem(lax.axis_index(ring) + 1, size)}
        sent.append(far(following, extra_ref, arrived_ids, 0))
        sent[0].start()
        spread(axis, picked_ref, column_block(width), full, *sems)

    square = jnp.zeros((slots, 1), f32)
    for i in range(0, model, columns):
        part = full[:, i : i + columns].astype(f32)
        square = square + jnp.sum(part * part, axis=1, keepdims=True)
    scale = lax.rsqrt(square / model + 1e-06)
    for i in range(0, model, columns):
        at = slice(i, i + columns)
        moe_in[:, at] = (full[:, at].astype(f32) * scale * gain_ref[:, at]).astype(bf16)

    def piece(i, carry):
        fetch_in(gate_hbm, gate, gate_sem, i).wait()
        gate_part = jnp.dot(moe_in[...], gate[i], preferred_element_type=f32)
        fetch_in(up_hbm, up, up_sem, i).wait()
        up_part = jnp.dot(moe_in[...], up[i], preferred_element_type=f32)
        at = pl.ds(pl.multiple_of(i * columns, columns), columns)
        hidden[:, at] = (gate_part * jax.nn.sigmoid(gate_part) * up_part).astype(bf16)
        return carry

    lax.fori_loop(0, pieces, piece, 0)

    def term(k):
        fetch_down(k).wait()
        return jnp.dot(hidden[...], down[k], preferred_element_type=f32)

    def to(peer, source, target, i, k):
        return pltpu.make_async_remote_copy(
            src_ref=source,
            dst_ref=target,
            send_sem=out_sem.at[i, k],
            recv_sem=in_sem.at[i, k],
            device_id={axis: peer},
            device_id_type=MESH,
        )

    half = model // 2

    def part_of(k, i):
        peer = lax.rem(me + k, n)
        if not last:
            return to(peer, terms.at[k], held.at[k], 0, k)
        at = pl.ds(i * half, half)
        return to(peer, terms.at[peer, :, at], held.at[k, :, at], i, k)

    def route():
        logits = lax.dot_general(
            moe_in[...], router_ref[...], (((1,), (1,)), ((), ())), preferred_element_type=f32
        )
        one = jax.nn.sigmoid(jnp.sum(logits * choice_ref[...], axis=1, keepdims=True))
        marks = marks_ref[...]
        return marks[:, 0:1] * one + marks[:, 1:2] * (1.0 - one)

    if last:
        capacity = slots // n

        def rows(q, carry):
            at = pl.ds(pl.multiple_of(q * width, width), width)
            terms[:, :, at] = term(q).reshape(n, capacity, width).astype(bf16)
            return carry

        for i in range(2):
            lax.fori_loop(i * n // 2, (i + 1) * n // 2, rows, 0)
            for k in range(1, n):
                part_of(k, i).start()
        route_ref[...] = route()
        total = terms[me].astype(f32)
        for k in range(1, n):
            for i in range(2):
                part_of(k, i).wait()
            total = total + held[k].astype(f32)
        o_ref[...] = total.astype(bf16)
    else:

        def block(k, carry):
            terms[k] = term(k).astype(bf16)
            part_of(k, 0).start()
            return carry

        lax.fori_loop(1, n, block, 0)
        total = term(0).astype(bf16).astype(f32)
        weight = route()
        for k in range(1, n):
            part_of(k, 0).wait()
            total = total + held[k].astype(f32)
        expert_out = total.astype(bf16).astype(f32)
        o_ref[...] = (picked_ref[...].astype(f32) + weight * expert_out).astype(bf16)
        sent.append(far(following, o_ref, arrived, 1))
        sent[1].start()
    for copy in sent:
        copy.wait()


def expert(picked, gain, router, choice, marks, extra, gate, up, down, last, axis, ring, cid):
    n = lax.axis_size(axis)
    slots, width = picked.shape
    model, ff = gate.shape
    columns = 512 if ff % 512 == 0 else ff
    f32, bf16 = jnp.float32, jnp.bfloat16
    dma = pltpu.SemaphoreType.DMA
    vmem = pl.BlockSpec(memory_space=pltpu.VMEM)
    hbm = pl.BlockSpec(memory_space=pltpu.HBM)
    part = (slots // n, model) if last else (slots, width)
    rows = jax.ShapeDtypeStruct(part, bf16)
    full = jax.ShapeDtypeStruct((slots, model), bf16)
    if last:
        moved = jax.ShapeDtypeStruct((extra.shape[0] // n, model), bf16)
        out_shape = [rows, jax.ShapeDtypeStruct((slots, 1), f32), full, moved]
    else:
        out_shape = [rows, full, rows, jax.ShapeDtypeStruct(extra.shape, extra.dtype)]
    return pl.pallas_call(
        functools.partial(expert_kernel, axis, ring, last, columns),
        out_shape=out_shape,
        in_specs=[vmem] * 6 + [hbm] * 3,
        out_specs=[vmem] * len(out_shape),
        scratch_shapes=[
            pltpu.VMEM((slots, model), bf16),
            pltpu.VMEM((slots, ff), bf16),
            pltpu.VMEM((ff // columns, model, columns), bf16),
            pltpu.VMEM((ff // columns, model, columns), bf16),
            pltpu.VMEM((n, ff, width), bf16),
            pltpu.VMEM((n,) + part, bf16),
            pltpu.VMEM((n,) + part, bf16),
            dma((ff // columns,)),
            dma((ff // columns,)),
            dma((n,)),
            dma((2, n)),
            dma((2, n)),
            dma((n,)),
            dma((n,)),
            dma,
        ]
        + spread_scratch(n),
        compiler_params=pltpu.CompilerParams(
            collective_id=cid, has_side_effects=True, vmem_limit_bytes=EXPERT_VMEM
        ),
        cost_estimate=pl.CostEstimate(
            flops=6 * slots * model * ff,
            bytes_accessed=6 * model * ff,
            transcendentals=slots * ff,
        ),
        name=f"expert_{cid}",
    )(picked, gain, router, choice, marks, extra, gate, up, down)


def passed_along(x, axis):
    length = lax.axis_size(axis)
    return lax.ppermute(x, axis, [(i, (i + 1) % length) for i in range(length)])


def dispatch_of(ids, blocks, capacity):
    length = ids.shape[0]
    size = length // blocks
    routed = (ids[:, 0] == 0) | (ids[:, 1] == 0)
    counted = routed.astype(jnp.float32).reshape(blocks, size)
    before = jnp.tril(jnp.ones((size, size), jnp.float32), -1)
    rank = jnp.dot(counted, before.T).reshape(length)
    slot = rank.astype(jnp.int32) + (jnp.arange(length, dtype=jnp.int32) // size) * capacity
    chosen = (jnp.arange(blocks * capacity, dtype=jnp.int32)[:, None] == slot[None, :]) & routed[
        None, :
    ]
    return chosen.astype(jnp.bfloat16), routed


def body(
    input_in_transit,
    mixer_norm_gain,
    convolution_weight,
    convolution_bias,
    input_projection,
    step_size_projection,
    step_size_bias,
    log_decay_rates,
    mixer_skip_weight,
    expert_norm_gain,
    router,
    gate_weight,
    up_weight,
    down_weight,
    expert_index_table,
):
    n, me = lax.axis_size("seq"), lax.axis_index("seq")
    experts = router.shape[2]
    rows = input_in_transit.shape[1]
    model = input_in_transit.shape[2]
    nstate = log_decay_rates.shape[2]
    rank = step_size_projection.shape[1]
    kernel = convolution_weight.shape[1]
    capacity = rows // 16
    length, width = rows * n, model // n
    slots = capacity * n
    f32, bf16 = jnp.float32, jnp.bfloat16

    def own(weight, axis):
        return lax.dynamic_slice_in_dim(weight, me * width, width, axis)

    gain = own(mixer_norm_gain[0], 0)
    taps = own(convolution_weight[0], 1)
    conv_bias = own(convolution_bias[0], 0)
    dt_bias = own(step_size_bias[0], 0)
    rates = -LOG2E * jnp.exp(own(log_decay_rates[0], 0)).T
    skip = own(mixer_skip_weight[0], 0)

    tokens = input_in_transit[0]
    as_float = tokens.astype(f32)
    square = jnp.sum(as_float * as_float, axis=-1)
    ids = expert_index_table[:, 0].astype(f32)
    small = jnp.concatenate(
        [ids.transpose(0, 2, 1).reshape(2 * STEPS, rows), square[None]], 0
    )
    small = jnp.pad(small, ((0, -small.shape[0] % ROWS), (0, 0)))
    small, present = exchange(
        [small, tokens],
        [(n,) + small.shape, (length, width)],
        [(whole, slot_of), (column_block(width), row_block(rows))],
        "seq",
        1,
    )
    square = small[:, 2 * STEPS].reshape(length)
    all_ids = small[:, : 2 * STEPS].reshape(n, STEPS, 2, rows).transpose(1, 0, 3, 2)
    all_ids = all_ids.reshape(STEPS, length, 2)
    for step in range(STEPS):
        if step:
            as_float = present.astype(f32)
            part = jnp.sum(as_float * as_float, axis=-1).reshape(n, rows)
            part = jnp.pad(part, ((0, -n % ROWS), (0, 0)))
            (part,) = exchange([part], [(n,) + part.shape], [(whole, slot_of)], "seq", 3)
            square = jnp.sum(part, axis=0)[:n].reshape(length)
        scale = lax.rsqrt(square / model + 1e-06)
        normed = (present.astype(f32) * scale[:, None] * gain).astype(bf16)
        padded = jnp.concatenate([jnp.zeros((kernel - 1, width), bf16), normed], 0)
        convolved = conv_bias
        for tap in range(kernel):
            convolved = convolved + taps[tap] * padded[tap : tap + length].astype(f32)
        inner = jax.nn.silu(convolved)
        inner_b = inner.astype(bf16)
        low = jnp.dot(
            inner_b, input_projection[0, :, :rank], preferred_element_type=f32
        ).astype(bf16)
        maps = lax.dot_general(
            input_projection[0, :, rank:],
            inner_b,
            (((0,), (1,)), ((), ())),
            preferred_element_type=f32,
        ).astype(bf16)
        mixed = mix(
            low,
            maps,
            inner,
            present,
            step_size_projection[0],
            dt_bias[None],
            rates,
            skip[None],
            "seq",
            4,
        )
        dispatch, routed = dispatch_of(all_ids[step], n, capacity)
        picked = jnp.dot(dispatch, mixed, preferred_element_type=f32).astype(bf16)
        last = step + 1 == STEPS
        if not last:
            moved = passed_along(mixed, "section")
        slot_ids = jnp.dot(dispatch, all_ids[step].astype(bf16), preferred_element_type=f32)
        one_hot = (
            slot_ids[:, :, None] == jnp.arange(experts, dtype=jnp.int32).astype(f32)
        ).astype(f32)
        choice = one_hot[:, 0] - one_hot[:, 1]
        is_first = slot_ids[:, 0] == 0
        is_second = (slot_ids[:, 1] == 0) & ~is_first
        marks = jnp.stack([is_first, is_second], 1).astype(f32)
        outs = expert(
            picked,
            expert_norm_gain,
            router[0].T,
            choice,
            marks,
            mixed if last else all_ids[step].T,
            gate_weight[0],
            up_weight[0],
            down_weight[0],
            last,
            "seq",
            "section",
            8 if last else 7,
        )
        if last:
            expert_out, route, full, mixed = outs
            dispatch = lax.dynamic_slice(
                dispatch, (me * capacity, me * rows), (capacity, rows)
            )
            routed = lax.dynamic_slice_in_dim(routed, me * rows, rows, 0)
            route = lax.dynamic_slice_in_dim(route, me * capacity, capacity, 0)
            picked = lax.dynamic_slice_in_dim(full, me * capacity, capacity, 0)
            new_rows = (picked.astype(f32) + route * expert_out.astype(f32)).astype(bf16)
        else:
            new_rows = outs[2]
            dispatch, routed = dispatch_of(outs[3].T, n, capacity)
            mixed = moved
        placed = lax.dot_general(
            dispatch, new_rows, (((0,), (0,)), ((), ())), preferred_element_type=f32
        ).astype(bf16)
        present = jnp.where(routed[:, None], placed, mixed)
    return present[None]


def solution(mesh):
    return jax.shard_map(
        body,
        mesh=mesh,
        in_specs=(
            P("section", "seq", None),
            P("section", None),
            P("section", None, None),
            P("section", None),
            P("section", "seq", None),
            P("section", None, "seq"),
            P("section", None),
            P("section", None, None),
            P("section", None),
            P("section", None),
            P("section", None, None),
            P("section", None, "seq"),
            P("section", None, "seq"),
            P("section", "seq", None),
            P(None, "section", "seq", None),
        ),
        out_specs=P("section", "seq", None),
        check_vma=False,
    )
```
